32 devices in a mesh: dp: 4 (over z), row: 4 (over y, core), col: 2 (over x).
Axes of the slice: x: 2, y: 2, z: 4, core: 2. Of those that a mesh axis runs over, the one named last changes fastest.
Arguments:
- block_input: bfloat16 [8, 1792, 1024], P('dp', None, ('row', 'col')), may hold values from -45 to 45
- segment_ids: int32 [8, 1792], P('dp'), may hold values from 0 to 3, never falling along the last dimension, each value on 1 to 896 neighbouring positions
- out_grad: bfloat16 [8, 1792, 1024], P('dp', None, ('row', 'col')), may hold values from -6 to 6
- in_weight: bfloat16 [3, 1024, 1024], P(None, 'col', 'row'), may hold values from -0.1875 to 0.1875
- out_weight: bfloat16 [1024, 1024], P('row', 'col'), may hold values from -0.375 to 0.375
- gate_weight: bfloat16 [1024, 4608], P('col', 'row'), may hold values from -0.1875 to 0.1875
- up_weight: bfloat16 [1024, 4608], P('col', 'row'), may hold values from -0.1875 to 0.1875
- down_weight: bfloat16 [4608, 1024], P('row', 'col'), may hold values from -0.1875 to 0.1875
- conv_weight: bfloat16 [3, 1024], P(None, ('row', 'col')), may hold values from -3.5 to 3.5
- mixer_norm_gain: float32 [1024], replicated, may hold values from 0.5 to 1.5
- feedforward_norm_gain: float32 [1024], replicated, may hold values from 0.5 to 1.5
Outputs:
- block_output: bfloat16 [8, 1792, 1024], P('dp', None, ('row', 'col'))
- block_input_gradient: float32 [8, 1792, 1024], P('dp', None, ('row', 'col'))
- grad_in_weight: float32 [3, 1024, 1024], P(None, 'col', 'row')
- grad_out_weight: float32 [1024, 1024], P('row', 'col')
- grad_gate_weight: float32 [1024, 4608], P('col', 'row')
- grad_up_weight: float32 [1024, 4608], P('col', 'row')
- grad_down_weight: float32 [4608, 1024], P('row', 'col')
- grad_conv_weight: float32 [3, 1024], P(None, ('row', 'col'))
- mixer_gain_gradient: float32 [1024], P(('row', 'col'))
- feedforward_gain_gradient: float32 [1024], P(('row', 'col'))
The draws below stay inside these ranges and needn't reach their ends.
Inputs may be any that keep to these rules, and one draw needn't show every extreme that they name: `segment_ids`: along each sequence the segment numbers never fall; a segment covers at most half of 1792 positions.
All inputs are finite; a program needn't handle non-finite values.
Results may differ from the reference program's by a relative error of at most 0.013.
Values may be sent and summed in bfloat16 or wider, within the bound.
No kernel may reach another device: no remote copies, remote signals or barrier semaphores. Data moves between devices by JAX's collectives and lax.ppermute only.
A program may use at most 256 MiB of HBM per device.

```python
import math
import jax
import jax.numpy as jnp
import numpy as np
from jax import lax

D = 1024
FF = 4608
SEQ = 1792
BATCH = 8


def draw_block_input(key, part):
    keys = jax.random.split(key, 3)
    ranked = jnp.arange(D, dtype=jnp.float32) / D
    col_scale = 10.0 ** (0.5 * ranked + 0.5 * jax.random.uniform(keys[1], (D,), jnp.float32))
    row_scale = 10.0 ** jax.random.uniform(keys[2], (BATCH, SEQ, 1), jnp.float32)
    base_value = jnp.clip(jax.random.normal(keys[0], (BATCH, SEQ, D), jnp.float32), -4.0, 4.0)
    return (0.1 * base_value * row_scale * col_scale).astype(jnp.bfloat16)


def levels(own_key, extent, pieces, low, top_value):
    factor_of = 1.0
    for position, parts in pieces:
        steps = jax.random.uniform(jax.random.fold_in(jax.random.fold_in(own_key, 6), position), (parts,), jnp.float32, low / len(pieces), top_value / len(pieces))
        factor_of = factor_of * jnp.repeat(jnp.exp(steps), extent[position] // parts).reshape((-1,) + (1,) * (len(extent) - 1 - position))
    return factor_of


def split_up(number_of, total, limit, slope):
    loads = [(1 << 20) // math.isqrt(grade ** slope) + 1 for grade in range(2, number_of + 1)]
    surplus, given = total - limit - (number_of - 1), [1] * (number_of - 1)
    while surplus > 0:
        movable = [i for i in range(number_of - 1) if given[i] < limit]
        pool, budget = sum([loads[i] for i in movable]), surplus
        for i in movable:
            more = min(limit - given[i], max(1, budget * loads[i] // pool), surplus)
            given[i] = given[i] + more
            surplus = surplus - more
    return np.array([limit] + given)


def ragged_sizes(own_key, count, total, most, slope):
    if count == 2:
        one = jax.random.randint(own_key, (), max(1, total - most), min(most, total - 1) + 1)
        return jnp.stack([one, total - one])
    sizes = jnp.asarray(split_up(count, total, most, slope), jnp.int32)
    twos = (count - 1) // 2
    giver, taker = sizes[1:1 + 2 * twos:2], sizes[2:2 + 2 * twos:2]
    room = jnp.minimum(giver - 1, most - taker)
    moved = jax.random.randint(jax.random.fold_in(own_key, 1), (twos,), 0, 1 << 20) % (room + 1)
    sizes = sizes.at[1:1 + 2 * twos:2].set(giver - moved).at[2:2 + 2 * twos:2].set(taker + moved)
    return sizes[jax.random.permutation(jax.random.fold_in(own_key, 2), count)]


def bell_draw(key, dims, scale, reach, cuts=(), kind=jnp.bfloat16):
    entries = scale * jax.random.normal(key, dims, jnp.float32)
    if cuts:
        entries = entries * levels(key, dims, cuts, -0.22, 0.18)
    return jnp.clip(entries, -reach, reach).astype(kind)


def setup_inputs(seed: int = 0) -> dict:
    arg_keys = jax.random.split(jax.random.key(seed), 12)
    block_input = draw_block_input(jax.random.fold_in(arg_keys[11], 71), 0)
    segment_ids = jax.vmap(lambda own: jnp.searchsorted(jnp.cumsum(ragged_sizes(own, max(3, SEQ // 448), SEQ, SEQ // 2, 0)), jnp.arange(SEQ), side="right"))(jax.random.split(arg_keys[1], BATCH)).reshape((BATCH, SEQ)).astype(jnp.int32)
    out_grad = bell_draw(arg_keys[2], (BATCH, SEQ, D), 1.0, 6.0, ((0, 4), (2, 8)))
    in_weight = bell_draw(arg_keys[3], (3, D, D), D ** -0.5, 0.1875, ((1, 2), (2, 4)))
    out_weight = bell_draw(arg_keys[4], (D, D), (D // 4) ** -0.5, 0.375, ((0, 4), (1, 2)))
    gate_weight = bell_draw(arg_keys[5], (D, FF), D ** -0.5, 0.1875, ((0, 2), (1, 4)))
    up_weight = bell_draw(arg_keys[6], (D, FF), D ** -0.5, 0.1875, ((0, 2), (1, 4)))
    down_weight = bell_draw(arg_keys[7], (FF, D), (FF // 4) ** -0.5, 0.1875, ((0, 4), (1, 2)))
    conv_weight = bell_draw(arg_keys[8], (3, D), 3 ** -0.5, 3.5, ((1, 8),))
    mixer_norm_gain = jnp.clip(1.0 + 0.1 * jax.random.normal(arg_keys[9], (D,), jnp.float32), 0.5, 1.5)
    feedforward_norm_gain = jnp.clip(1.0 + 0.1 * jax.random.normal(arg_keys[10], (D,), jnp.float32), 0.5, 1.5)
    return dict(block_input=block_input, segment_ids=segment_ids, out_grad=out_grad, in_weight=in_weight, out_weight=out_weight, gate_weight=gate_weight, up_weight=up_weight, down_weight=down_weight, conv_weight=conv_weight, mixer_norm_gain=mixer_norm_gain, feedforward_norm_gain=feedforward_norm_gain)


EPS = 1e-05

def matmul(left_side, right_side):
    return jnp.dot(left_side, right_side, preferred_element_type=jnp.float32)

def lagged(values, shift_by):
    padding = jnp.zeros_like(values[..., :shift_by, :])
    return jnp.concatenate([padding, values[..., :-shift_by, :]], axis=-2)

def leading(values, shift_by):
    padding = jnp.zeros_like(values[..., :shift_by, :])
    return jnp.concatenate([values[..., shift_by:, :], padding], axis=-2)

def same_masks(segments):
    mask_list = []
    for shift_by in (1, 2):
        filler = jnp.full(segments[..., :shift_by].shape, -1, jnp.int32)
        earlier = jnp.concatenate([filler, segments[..., :-shift_by]], axis=-1)
        mask_list.append(jnp.where(earlier == segments, 1.0, 0.0).astype(jnp.float32)[..., None])
    return mask_list

def conv_forward(mixed_in, mask_list, kernel):
    return kernel[0] * mixed_in + kernel[1] * mask_list[0] * lagged(mixed_in, 1) + kernel[2] * mask_list[1] * lagged(mixed_in, 2)

def conv_backward(d_conved, mixed_in, mask_list, kernel):
    first_term = mask_list[0] * d_conved
    second = mask_list[1] * d_conved
    d_mixed = kernel[0] * d_conved + kernel[1] * leading(first_term, 1) + kernel[2] * leading(second, 2)
    all_axes = tuple(range(d_conved.ndim - 1))
    d_kernel = jnp.stack([lax.optimization_barrier(jnp.sum(d_conved * mixed_in, axis=all_axes)), lax.optimization_barrier(jnp.sum(first_term * lagged(mixed_in, 1), axis=all_axes)), lax.optimization_barrier(jnp.sum(second * lagged(mixed_in, 2), axis=all_axes))])
    return (d_mixed, d_kernel)

def rms_norm_backward(d_normed, x_hat, scale_row, gain_row):
    d_hat = d_normed * gain_row
    return scale_row * (d_hat - x_hat * lax.optimization_barrier(jnp.mean(d_hat * x_hat, axis=-1, keepdims=True)))

def reference(block_input, segment_ids, out_grad, in_weight, out_weight, gate_weight, up_weight, down_weight, conv_weight, mixer_norm_gain, feedforward_norm_gain):
    kernel = conv_weight.astype(jnp.float32)

    def one_sequence(totals, inputs):
        tokens, segments, upstream_gradient = inputs
        complete_input = tokens.astype(jnp.float32)
        mixer_inverse_scale = lax.rsqrt(lax.optimization_barrier(jnp.mean(complete_input * complete_input, axis=-1, keepdims=True)) + EPS)
        mixer_normalized = complete_input * mixer_inverse_scale
        mixer_normed = (mixer_normalized * mixer_norm_gain).astype(jnp.bfloat16)
        b_proj = matmul(mixer_normed, in_weight[0])
        c_proj = matmul(mixer_normed, in_weight[1])
        x_proj = matmul(mixer_normed, in_weight[2])
        mask_list = same_masks(segments)
        mixed_in = b_proj * x_proj
        conved = conv_forward(mixed_in, mask_list, kernel)
        gated_out = (c_proj * conved).astype(jnp.bfloat16)
        middle_residual = complete_input + matmul(gated_out, out_weight)
        feedforward_inverse_scale = lax.rsqrt(lax.optimization_barrier(jnp.mean(middle_residual * middle_residual, axis=-1, keepdims=True)) + EPS)
        feedforward_normalized = middle_residual * feedforward_inverse_scale
        feedforward_normed = (feedforward_normalized * feedforward_norm_gain).astype(jnp.bfloat16)
        gate_pre = matmul(feedforward_normed, gate_weight)
        up_pre = matmul(feedforward_normed, up_weight)
        sigmoid = jax.nn.sigmoid(gate_pre)
        activated = (gate_pre * sigmoid * up_pre).astype(jnp.bfloat16)
        output = (middle_residual + matmul(activated, down_weight)).astype(jnp.bfloat16)
        d_act = matmul(upstream_gradient, down_weight.T)
        grad_down = matmul(activated.T, upstream_gradient)
        d_up = (d_act * gate_pre * sigmoid).astype(jnp.bfloat16)
        d_gate = (d_act * up_pre * sigmoid * (1.0 + gate_pre * (1.0 - sigmoid))).astype(jnp.bfloat16)
        grad_gate = matmul(feedforward_normed.T, d_gate)
        grad_up = matmul(feedforward_normed.T, d_up)
        feedforward_normed_gradient = matmul(d_gate, gate_weight.T) + matmul(d_up, up_weight.T)
        feedforward_gain_gradient = lax.optimization_barrier(jnp.sum(feedforward_normed_gradient * feedforward_normalized, axis=0))
        residual_gradient = upstream_gradient.astype(jnp.float32) + rms_norm_backward(feedforward_normed_gradient, feedforward_normalized, feedforward_inverse_scale, feedforward_norm_gain)
        d_resid_half = residual_gradient.astype(jnp.bfloat16)
        grad_out = matmul(gated_out.T, d_resid_half)
        d_gated = matmul(d_resid_half, out_weight.T)
        d_cproj = (d_gated * conved).astype(jnp.bfloat16)
        d_conved = d_gated * c_proj
        d_mixed, grad_kernel = conv_backward(d_conved, mixed_in, mask_list, kernel)
        d_bproj = (d_mixed * x_proj).astype(jnp.bfloat16)
        d_xproj = (d_mixed * b_proj).astype(jnp.bfloat16)
        grad_in = jnp.stack([matmul(mixer_normed.T, d_bproj), matmul(mixer_normed.T, d_cproj), matmul(mixer_normed.T, d_xproj)])
        mixer_normed_gradient = matmul(d_bproj, in_weight[0].T) + matmul(d_cproj, in_weight[1].T) + matmul(d_xproj, in_weight[2].T)
        mixer_gain_gradient = lax.optimization_barrier(jnp.sum(mixer_normed_gradient * mixer_normalized, axis=0))
        block_input_gradient = residual_gradient + rms_norm_backward(mixer_normed_gradient, mixer_normalized, mixer_inverse_scale, mixer_norm_gain)
        updated = (totals[0] + grad_in, totals[1] + grad_out, totals[2] + grad_gate, totals[3] + grad_up, totals[4] + grad_down, totals[5] + grad_kernel, totals[6] + mixer_gain_gradient, totals[7] + feedforward_gain_gradient)
        return (updated, (output, block_input_gradient))
    zero_grads = (jnp.zeros(in_weight.shape, jnp.float32), jnp.zeros(out_weight.shape, jnp.float32), jnp.zeros(gate_weight.shape, jnp.float32), jnp.zeros(up_weight.shape, jnp.float32), jnp.zeros(down_weight.shape, jnp.float32), jnp.zeros(conv_weight.shape, jnp.float32), jnp.zeros(mixer_norm_gain.shape, jnp.float32), jnp.zeros(feedforward_norm_gain.shape, jnp.float32))
    totals, stacked = lax.scan(one_sequence, zero_grads, (block_input, segment_ids, out_grad))
    return (stacked[0], stacked[1], totals[0], totals[1], totals[2], totals[3], totals[4], totals[5], totals[6], totals[7])
```

```python
import jax
import jax.numpy as jnp
from jax import lax
from jax.sharding import PartitionSpec as P

EPS = 1e-05
F32 = jnp.float32
BF16 = jnp.bfloat16


def dot(left, right):
    return lax.dot_general(left, right, (((1,), (0,)), ((), ())), preferred_element_type=F32)


def dot_nt(left, right):
    return lax.dot_general(left, right, (((1,), (1,)), ((), ())), preferred_element_type=F32)


def dot_tn(left, right):
    return lax.dot_general(left, right, (((0,), (0,)), ((), ())), preferred_element_type=F32)


def rounded(values):
    return lax.reduce_precision(values, exponent_bits=8, mantissa_bits=7)


def in_order(first_is_mine, mine, other, axis):
    return jnp.where(
        first_is_mine,
        jnp.concatenate([mine, other], axis=axis),
        jnp.concatenate([other, mine], axis=axis),
    )


def swap_halves(values, axis):
    low, high = jnp.split(values, 2, axis=axis)
    return jnp.concatenate([high, low], axis=axis)


def rows_of(values, index, count):
    return lax.dynamic_slice_in_dim(values, index * count, count, axis=0)


def cols_of(values, index, count):
    return lax.dynamic_slice_in_dim(values, index * count, count, axis=1)


def to_col(values):
    size = lax.axis_size("col")
    return lax.ppermute(values, "col", [(i, size - 1 - i) for i in range(size)])


def to_core(values):
    size = lax.axis_size("row")
    return lax.ppermute(values, "row", [(i, i ^ 1) for i in range(size)])


def to_half(values):
    size = lax.axis_size("row")
    return lax.ppermute(values, "row", [(i, (i + size // 2) % size) for i in range(size)])


def line_sum(values, dtype):
    size = lax.axis_size("dp")
    place = lax.axis_index("dp")
    middle = size // 2
    keep = rounded if dtype == BF16 else (lambda v: v)
    total = values
    for step in range(middle - 1):
        pairs = [(step, step + 1), (size - 1 - step, size - 2 - step)]
        total = total + lax.ppermute(keep(total).astype(dtype), "dp", pairs).astype(F32)
    half = keep(total)
    total = keep(
        half
        + lax.ppermute(half.astype(dtype), "dp", [(middle - 1, middle), (middle, middle - 1)]).astype(F32)
    )
    for step in range(middle - 1):
        pairs = [(middle - 1 - step, middle - 2 - step), (middle + step, middle + step + 1)]
        got = lax.ppermute(total.astype(dtype), "dp", pairs).astype(F32)
        taker = (place == middle - 2 - step) | (place == middle + step + 1)
        total = jnp.where(taker, got, total)
    return total


def body(
    block_input,
    segment_ids,
    out_grad,
    in_weight,
    out_weight,
    gate_weight,
    up_weight,
    down_weight,
    conv_weight,
    mixer_norm_gain,
    feedforward_norm_gain,
):
    seq_count, seq_length, own_width = block_input.shape
    if lax.axis_size("row") != 4 or lax.axis_size("col") != 2 or seq_count != 2:
        raise ValueError("unsupported mesh")
    row = lax.axis_index("row")
    col = lax.axis_index("col")
    part = row // 2
    core = row % 2
    span = seq_length // 2
    home = span // 2
    width = mixer_norm_gain.shape[0]
    half_width = width // 2
    own_half_first = part == col
    core_low = core == 0
    part_low = part == 0
    col_low = col == 0

    def local_gain(gain):
        return jnp.concatenate(
            [
                lax.dynamic_slice_in_dim(gain, col * half_width, half_width),
                lax.dynamic_slice_in_dim(gain, (1 - col) * half_width, half_width),
            ]
        )

    def gather_span(values):
        mine = lax.dynamic_index_in_dim(values, col, 0, keepdims=False)
        other = lax.dynamic_index_in_dim(values, 1 - col, 0, keepdims=False)
        pair = in_order(col_low, mine, to_col(other), 1)
        quad = in_order(core_low, rows_of(pair, core, span), to_core(rows_of(pair, 1 - core, span)), 1)
        return quad, to_half(quad)

    def scatter_span(values):
        wide = 2 * own_width
        mine = cols_of(values, core, wide)
        got = to_core(cols_of(values, 1 - core, wide).astype(BF16)).astype(values.dtype)
        pair = in_order(core_low, mine, got, 0)
        mine = cols_of(pair, col, own_width)
        got = to_col(cols_of(pair, 1 - col, own_width).astype(BF16)).astype(values.dtype)
        return in_order(col_low, mine[None], got[None], 0)

    def local_features(mine, other):
        return jnp.concatenate(
            [jnp.where(own_half_first, mine, other), jnp.where(own_half_first, other, mine)], axis=1
        )

    input_half, input_other = gather_span(block_input)

    mixer_in = jnp.concatenate([in_weight, to_col(in_weight)], axis=1)
    mixer_in = jnp.concatenate([mixer_in, to_core(mixer_in)], axis=2)
    mixer_out = jnp.concatenate([out_weight, to_col(out_weight)], axis=1)
    mixer_out = jnp.concatenate([mixer_out, to_core(mixer_out)], axis=0)
    kernel = in_order(col_low, conv_weight, to_col(conv_weight), 1)
    kernel = jnp.concatenate([kernel, to_core(kernel)], axis=1).astype(F32)
    gate_all = jnp.concatenate([gate_weight, to_col(gate_weight)], axis=0)
    gate_all = jnp.concatenate([gate_all, to_core(gate_all)], axis=1)
    up_all = jnp.concatenate([up_weight, to_col(up_weight)], axis=0)
    up_all = jnp.concatenate([up_all, to_core(up_all)], axis=1)
    cot_half, cot_other = gather_span(out_grad)
    down_all = jnp.concatenate([down_weight, to_col(down_weight)], axis=1)
    down_all = jnp.concatenate([down_all, to_core(down_all)], axis=0)
    hidden = gate_weight.shape[1]
    channels = in_weight.shape[2]

    gain_one = local_gain(mixer_norm_gain)
    gain_two = local_gain(feedforward_norm_gain)

    segments = lax.dynamic_index_in_dim(segment_ids, col, 0, keepdims=False)

    def same_as(lag):
        earlier = jnp.concatenate([jnp.full((lag,), -1, jnp.int32), segments[:-lag]])
        return rows_of(jnp.where(earlier == segments, 1.0, 0.0).astype(F32), core, span)[:, None]

    mask_one, mask_two = same_as(1), same_as(2)

    inputs = local_features(input_half, input_other).astype(F32)
    scale_one = lax.rsqrt(jnp.mean(inputs * inputs, axis=1, keepdims=True) + EPS)
    normed_one = (inputs * scale_one * gain_one).astype(BF16)
    projected = jnp.einsum("td,jdc->jtc", normed_one, mixer_in, preferred_element_type=F32)
    b_proj, c_proj, x_proj = projected[0], projected[1], projected[2]
    mixed_in = b_proj * x_proj
    before = jnp.where(core_low, 0.0, swap_halves(to_core(mixed_in[-2:]), 1))
    extended = jnp.concatenate([before, mixed_in], axis=0)
    lag_one, lag_two = extended[1:-1], extended[:-2]
    conved = kernel[0] * mixed_in + kernel[1] * mask_one * lag_one + kernel[2] * mask_two * lag_two
    gated_out = (c_proj * conved).astype(BF16)
    mixer_got = to_half(dot(rows_of(gated_out, 1 - part, home), mixer_out).astype(BF16))
    resid_mid = (
        rows_of(inputs, part, home) + dot(rows_of(gated_out, part, home), mixer_out) + mixer_got.astype(F32)
    )

    scale_two = lax.rsqrt(jnp.mean(resid_mid * resid_mid, axis=1, keepdims=True) + EPS)
    hat_two = resid_mid * scale_two
    normed_own = (hat_two * gain_two).astype(BF16)
    normed_two = jnp.concatenate([normed_own, to_half(normed_own)], axis=0)
    slot = jnp.where(own_half_first, 0, 1)
    resid_got = to_half(cols_of(resid_mid, 1 - slot, half_width).astype(BF16))
    cot_span = local_features(cot_half, cot_other)
    cotangent = jnp.concatenate([rows_of(cot_span, part, home), rows_of(cot_span, 1 - part, home)], axis=0)
    gate_pre = dot(normed_two, gate_all)
    up_pre = dot(normed_two, up_all)
    sigmoid = jax.nn.sigmoid(gate_pre)
    activated = (gate_pre * sigmoid * up_pre).astype(BF16)
    d_act = dot_nt(cotangent, down_all)
    d_up = (d_act * gate_pre * sigmoid).astype(BF16)
    d_gate = (d_act * up_pre * sigmoid * (1.0 + gate_pre * (1.0 - sigmoid))).astype(BF16)
    d_normed_got = to_half((dot_nt(d_gate[home:], gate_all) + dot_nt(d_up[home:], up_all)).astype(BF16))
    d_normed = dot_nt(d_gate[:home], gate_all) + dot_nt(d_up[:home], up_all) + d_normed_got.astype(F32)

    def to_grid_by_column(left, right, count):
        from_core = to_core(dot_tn(left, right[:, count:]).astype(BF16)).astype(F32)
        mine = right[:, :count]
        low, high = left[:, :half_width], left[:, half_width:]
        from_col = to_col((dot_tn(high, mine) + from_core[half_width:]).astype(BF16)).astype(F32)
        return line_sum(dot_tn(low, mine) + from_core[:half_width] + from_col, BF16)

    def to_grid_by_row(left, right, count):
        from_core = to_core(dot_tn(left[:, count:], right).astype(BF16)).astype(F32)
        mine = left[:, :count]
        low, high = right[:, :half_width], right[:, half_width:]
        from_col = to_col((dot_tn(mine, high) + from_core[:, half_width:]).astype(BF16)).astype(F32)
        return line_sum(dot_tn(mine, low) + from_core[:, :half_width] + from_col, BF16)

    grad_down = to_grid_by_row(activated, cotangent, hidden)
    grad_gate = to_grid_by_column(normed_two, d_gate, hidden)
    grad_up = to_grid_by_column(normed_two, d_up, hidden)

    gain_two_sum = jnp.sum(d_normed * hat_two, axis=0)
    d_hat = d_normed * gain_two
    mean_two = jnp.mean(d_hat * hat_two, axis=1, keepdims=True)
    d_resid = (cotangent[:home].astype(F32) + scale_two * (d_hat - hat_two * mean_two)).astype(BF16)
    d_resid_span = in_order(part_low, d_resid, to_half(d_resid), 0)

    down_mine = cols_of(down_all, slot, half_width)
    down_other = cols_of(down_all, 1 - slot, half_width)
    output_got = swap_halves(to_half(dot(activated, down_other).astype(BF16)), 0).astype(F32)
    resid_half = jnp.concatenate([cols_of(resid_mid, slot, half_width), resid_got.astype(F32)], axis=0)
    output_half = (dot(activated, down_mine) + output_got + resid_half).astype(BF16)
    output_half = jnp.where(part_low, output_half, swap_halves(output_half, 0))
    block_output = scatter_span(output_half)

    d_gated = dot_nt(d_resid_span, mixer_out)
    grad_out = to_grid_by_row(gated_out, d_resid_span, channels)
    d_cproj = (d_gated * conved).astype(BF16)
    d_conved = d_gated * c_proj
    first_term = mask_one * d_conved
    second = mask_two * d_conved
    edge = to_core(jnp.concatenate([first_term[:1], second[:2]], axis=0))
    edge = jnp.where(core_low, swap_halves(edge, 1), 0.0)
    d_mixed = (
        kernel[0] * d_conved
        + kernel[1] * jnp.concatenate([first_term[1:], edge[:1]], axis=0)
        + kernel[2] * jnp.concatenate([second[2:], edge[1:]], axis=0)
    )
    kernel_sum = jnp.stack(
        [
            jnp.sum(d_conved * mixed_in, axis=0),
            jnp.sum(first_term * lag_one, axis=0),
            jnp.sum(second * lag_two, axis=0),
        ]
    )
    d_bproj = (d_mixed * x_proj).astype(BF16)
    d_xproj = (d_mixed * b_proj).astype(BF16)
    d_projected = jnp.stack([d_bproj, d_cproj, d_xproj])

    def input_gradient(index):
        weights = lax.dynamic_slice_in_dim(mixer_in, index * half_width, half_width, axis=1)
        return jnp.einsum("jtc,jdc->td", d_projected, weights, preferred_element_type=F32)

    one_got = to_half(input_gradient(1 - slot).astype(BF16))
    d_normed_one = input_gradient(slot) + one_got.astype(F32)

    def in_piece(left, pieces):
        return jnp.einsum("td,jtc->jdc", left, pieces, preferred_element_type=F32)

    from_core = to_core(in_piece(normed_one, d_projected[:, :, channels:]).astype(BF16)).astype(F32)
    mine = d_projected[:, :, :channels]
    from_col = to_col(
        (in_piece(normed_one[:, half_width:], mine) + from_core[:, half_width:]).astype(BF16)
    ).astype(F32)
    grad_in = line_sum(
        in_piece(normed_one[:, :half_width], mine) + from_core[:, :half_width] + from_col, BF16
    )

    hat_one = input_half.astype(F32) * scale_one
    gain_half = lax.dynamic_slice_in_dim(mixer_norm_gain, part * half_width, half_width)
    gain_one_sum = jnp.sum(d_normed_one * hat_one, axis=0)
    d_hat_one = d_normed_one * gain_half
    stat = jnp.sum(d_hat_one * hat_one, axis=1)
    mean_one = ((stat + to_half(stat)) / width)[:, None]
    d_input = cols_of(d_resid_span, slot, half_width).astype(F32) + scale_one * (d_hat_one - hat_one * mean_one)
    block_input_gradient = scatter_span(d_input)

    kernel_sum = jnp.where(core_low, kernel_sum, swap_halves(kernel_sum, 1))
    halves = jnp.concatenate([kernel_sum, gain_one_sum[None]], axis=0)
    wide = in_order(part_low, halves, jnp.zeros_like(halves), 1)
    two = gain_two_sum[None]
    small = jnp.concatenate([wide, jnp.where(col_low, two, swap_halves(two, 1))], axis=0)
    small = small + to_core(small)
    small = small + to_col(small)
    small = small + to_half(small)
    small = line_sum(small, F32)
    small = lax.dynamic_slice_in_dim(small, (row * 2 + col) * own_width, own_width, axis=1)

    return (
        block_output,
        block_input_gradient,
        grad_in,
        grad_out,
        grad_gate,
        grad_up,
        grad_down,
        small[:3],
        small[3],
        small[4],
    )


def solution(mesh):
    placed = (
        P("dp", None, ("row", "col")),
        P("dp", None),
        P("dp", None, ("row", "col")),
        P(None, "col", "row"),
        P("row", "col"),
        P("col", "row"),
        P("col", "row"),
        P("row", "col"),
        P(None, ("row", "col")),
        P(),
        P(),
    )
    return jax.shard_map(
        body,
        mesh=mesh,
        in_specs=placed,
        out_specs=(
            P("dp", None, ("row", "col")),
            P("dp", None, ("row", "col")),
            P(None, "col", "row"),
            P("row", "col"),
            P("col", "row"),
            P("col", "row"),
            P("row", "col"),
            P(None, ("row", "col")),
            P(("row", "col")),
            P(("row", "col")),
        ),
        check_vma=False,
    )
```

```python
import jax
import jax.numpy as jnp
from jax import lax
from jax.sharding import PartitionSpec as P


EPS = 1e-05
F32 = jnp.float32
BF16 = jnp.bfloat16


def contract(left, right, left_axis, right_axis):
    return lax.dot_general(
        left, right, (((left_axis,), (right_axis,)), ((), ())), preferred_element_type=F32
    )


def dot(left, right):
    return contract(left, right, 1, 0)


def dot_nt(left, right):
    return contract(left, right, 1, 1)


def dot_tn(left, right):
    return contract(left, right, 0, 0)


def rounded(values):
    return lax.reduce_precision(values, exponent_bits=8, mantissa_bits=7)


def in_order(first_is_mine, mine, other, axis):
    return jnp.where(
        first_is_mine,
        jnp.concatenate([mine, other], axis=axis),
        jnp.concatenate([other, mine], axis=axis),
    )


def swap_halves(values, axis):
    low, high = jnp.split(values, 2, axis=axis)
    return jnp.concatenate([high, low], axis=axis)


def rows_of(values, index, count):
    return lax.dynamic_slice_in_dim(values, index * count, count, axis=0)


def cols_of(values, index, count):
    return lax.dynamic_slice_in_dim(values, index * count, count, axis=1)


def after(values, *others):
    return lax.optimization_barrier((values, *others))[0]


def pad_rows(values, before, behind):
    return jnp.pad(values, ((before, behind), (0, 0)))


def to_col(values):
    size = lax.axis_size("col")
    return lax.ppermute(values, "col", [(i, size - 1 - i) for i in range(size)])


def to_core(values):
    size = lax.axis_size("row")
    return lax.ppermute(values, "row", [(i, i ^ 1) for i in range(size)])


def to_half(values):
    size = lax.axis_size("row")
    return lax.ppermute(values, "row", [(i, (i + size // 2) % size) for i in range(size)])


def line_sum(values, dtype, middle_after=(), outward_after=()):
    size = lax.axis_size("dp")
    place = lax.axis_index("dp")
    middle = size // 2
    keep = rounded if dtype == BF16 else (lambda v: v)
    total = values
    for step in range(middle - 1):
        pairs = [(step, step + 1), (size - 1 - step, size - 2 - step)]
        got = after(lax.ppermute(keep(total).astype(dtype), "dp", pairs), *middle_after)
        total = total + got.astype(F32)
    half = keep(total).astype(dtype)
    pairs = [(middle - 1, middle), (middle, middle - 1)]
    got = after(lax.ppermute(half, "dp", pairs), *outward_after)
    whole = keep(keep(total) + got.astype(F32)).astype(dtype)
    result = whole
    for step in range(middle - 1):
        pairs = [(middle - 1 - step, middle - 2 - step), (middle + step, middle + step + 1)]
        got = lax.ppermute(result, "dp", pairs)
        taker = (place == middle - 2 - step) | (place == middle + step + 1)
        result = jnp.where(taker, got, result)
    return result.astype(F32), half, whole


def body(
    block_input,
    segment_ids,
    out_grad,
    in_weight,
    out_weight,
    gate_weight,
    up_weight,
    down_weight,
    conv_weight,
    mixer_norm_gain,
    feedforward_norm_gain,
):
    seq_count, seq_length, own_width = block_input.shape
    if lax.axis_size("row") != 4 or lax.axis_size("col") != 2 or seq_count != 2 or lax.axis_size("dp") % 2:
        raise ValueError("unsupported mesh")
    row = lax.axis_index("row")
    col = lax.axis_index("col")
    part = row >> 1
    core = row & 1
    span = seq_length // 2
    home = span // 2
    width = mixer_norm_gain.shape[0]
    half_width = width // 2
    own_half_first = part == col
    core_low = core == 0
    part_low = part == 0
    col_low = col == 0

    def local_gain(gain):
        return jnp.concatenate(
            [
                lax.dynamic_slice_in_dim(gain, col * half_width, half_width),
                lax.dynamic_slice_in_dim(gain, (1 - col) * half_width, half_width),
            ]
        )

    def scatter_span(values):
        wide = 2 * own_width
        mine = cols_of(values, core, wide)
        got = to_core(cols_of(values, 1 - core, wide).astype(BF16)).astype(values.dtype)
        pair = in_order(core_low, mine, got, 0)
        mine = cols_of(pair, col, own_width)
        got = to_col(cols_of(pair, 1 - col, own_width).astype(BF16)).astype(values.dtype)
        return in_order(col_low, mine[None], got[None], 0)

    def local_features(mine, other):
        return jnp.concatenate(
            [jnp.where(own_half_first, mine, other), jnp.where(own_half_first, other, mine)], axis=1
        )

    def of_sequence(values, index):
        return lax.dynamic_index_in_dim(values, index, 0, keepdims=False)

    def gather_span(values, got):
        pair = in_order(col_low, of_sequence(values, col), got, 1)
        got = to_core(rows_of(pair, 1 - core, span))
        quad = in_order(core_low, rows_of(pair, core, span), got, 1)
        return quad, to_half(quad)

    input_got = to_col(of_sequence(block_input, 1 - col))
    input_half, input_other = gather_span(block_input, input_got)

    mixer_in = jnp.concatenate([in_weight, to_col(in_weight)], axis=1)
    mixer_in = jnp.concatenate([mixer_in, to_core(mixer_in)], axis=2)
    mixer_out = jnp.concatenate([out_weight, to_col(out_weight)], axis=1)
    mixer_out = jnp.concatenate([mixer_out, to_core(mixer_out)], axis=0)
    kernel = in_order(col_low, conv_weight, to_col(conv_weight), 1)
    kernel = jnp.concatenate([kernel, to_core(kernel)], axis=1).astype(F32)

    gate_got = to_col(gate_weight)
    cot_got = to_col(of_sequence(out_grad, 1 - col))
    up_got, down_got = to_col(up_weight), to_col(down_weight)
    hidden = gate_weight.shape[1]
    channels = in_weight.shape[2]

    gain_one = local_gain(mixer_norm_gain)
    gain_two = local_gain(feedforward_norm_gain)

    segments = lax.dynamic_index_in_dim(segment_ids, col, 0, keepdims=False)

    def same_as(lag):
        earlier = jnp.concatenate([jnp.full((lag,), -1, jnp.int32), segments[:-lag]])
        return rows_of(jnp.where(earlier == segments, 1.0, 0.0).astype(F32), core, span)[:, None]

    mask_one, mask_two = same_as(1), same_as(2)

    inputs = local_features(input_half, input_other).astype(F32)
    scale_one = lax.rsqrt(jnp.mean(inputs * inputs, axis=1, keepdims=True) + EPS)
    normed_one = (inputs * scale_one * gain_one).astype(BF16)
    projected = jnp.einsum("td,jdc->jtc", normed_one, mixer_in, preferred_element_type=F32)
    b_proj, c_proj, x_proj = projected[0], projected[1], projected[2]
    mixed_in = b_proj * x_proj
    edge_rows = 8
    rest = span - edge_rows
    before = jnp.where(core_low, 0.0, swap_halves(to_core(mixed_in[rest:]), 1))
    before_one = pad_rows(before[edge_rows - 1 :], 0, edge_rows - 1)
    before_two = pad_rows(before[edge_rows - 2 :], 0, edge_rows - 2)
    lag_one, lag_two = pad_rows(mixed_in[:-1], 1, 0), pad_rows(mixed_in[:-2], 2, 0)
    from_before = (
        kernel[1] * mask_one[:edge_rows] * before_one + kernel[2] * mask_two[:edge_rows] * before_two
    )
    conved = (
        kernel[0] * mixed_in
        + kernel[1] * mask_one * lag_one
        + kernel[2] * mask_two * lag_two
        + pad_rows(from_before, 0, rest)
    )
    gated_out = (c_proj * conved).astype(BF16)
    mixer_send = dot(rows_of(gated_out, 1 - part, home), mixer_out).astype(BF16)
    mixer_got = to_half(mixer_send)
    gate_all = jnp.concatenate([gate_weight, after(gate_got, mixer_send)], axis=0)
    gate_all = jnp.concatenate([gate_all, to_core(gate_all)], axis=1)
    resid_mid = rows_of(inputs, part, home) + dot(rows_of(gated_out, part, home), mixer_out) + mixer_got.astype(F32)

    scale_two = lax.rsqrt(jnp.mean(resid_mid * resid_mid, axis=1, keepdims=True) + EPS)
    hat_two = resid_mid * scale_two
    normed_own = (hat_two * gain_two).astype(BF16)
    normed_other = to_half(normed_own)
    cot_half, cot_other = gather_span(out_grad, after(cot_got, normed_own))
    normed_two = jnp.concatenate([normed_own, normed_other], axis=0)
    slot = jnp.where(own_half_first, 0, 1)
    resid_got = to_half(cols_of(resid_mid, 1 - slot, half_width).astype(BF16))
    gate_pre = dot(normed_two, gate_all)
    up_all = jnp.concatenate([up_weight, after(up_got, gate_pre)], axis=0)
    up_all = jnp.concatenate([up_all, to_core(up_all)], axis=1)
    up_pre = dot(normed_two, up_all)
    sigmoid = jax.nn.sigmoid(gate_pre)
    activated = (gate_pre * sigmoid * up_pre).astype(BF16)
    down_all = jnp.concatenate([down_weight, after(down_got, activated)], axis=1)
    down_all = jnp.concatenate([down_all, to_core(down_all)], axis=0)
    cot_span = local_features(cot_half, after(cot_other, activated))
    cotangent = jnp.concatenate([rows_of(cot_span, part, home), rows_of(cot_span, 1 - part, home)], axis=0)

    def finish(low, from_core, from_col):
        return low + from_core.astype(F32) + from_col.astype(F32)

    down_core = to_core(dot_tn(activated[:, hidden:], cotangent).astype(BF16))
    activated_mine = activated[:, :hidden]
    down_high = dot_tn(activated_mine, cotangent[:, half_width:])
    down_high = (down_high + down_core[:, half_width:].astype(F32)).astype(BF16)
    down_col = to_col(down_high)

    down_mine = cols_of(down_all, slot, half_width)
    down_other = cols_of(down_all, 1 - slot, half_width)
    output_send = dot(activated, down_other).astype(BF16)
    output_got = to_half(output_send)

    d_act = dot_nt(after(cotangent, down_high, output_send), down_all)
    d_up = (d_act * gate_pre * sigmoid).astype(BF16)
    d_gate = (d_act * up_pre * sigmoid * (1.0 + gate_pre * (1.0 - sigmoid))).astype(BF16)

    low, high = normed_two[:, :half_width], normed_two[:, half_width:]
    gate_core = to_core(dot_tn(normed_two, d_gate[:, hidden:]).astype(BF16))
    up_core = to_core(dot_tn(normed_two, d_up[:, hidden:]).astype(BF16))
    gate_mine, up_mine = d_gate[:, :hidden], d_up[:, :hidden]
    gate_high = dot_tn(high, gate_mine)
    gate_high = (gate_high + gate_core[half_width:].astype(F32)).astype(BF16)
    gate_col = to_col(gate_high)
    up_high = (dot_tn(high, up_mine) + up_core[half_width:].astype(F32)).astype(BF16)
    up_col = to_col(up_high)

    down_sum = finish(
        dot_tn(activated_mine, after(cotangent, up_high)[:, :half_width]),
        down_core[:, :half_width],
        after(down_col, up_high),
    )

    d_gate_late, d_up_late = after(d_gate, up_high), after(d_up, up_high)

    def normed_gradient(rows):
        return dot_nt(d_gate_late[rows], gate_all) + dot_nt(d_up_late[rows], up_all)

    d_normed_send = normed_gradient(slice(home, None)).astype(BF16)
    d_normed_got = to_half(d_normed_send)
    gate_sum = finish(
        dot_tn(after(low, d_normed_send), gate_mine), gate_core[:half_width], after(gate_col, d_normed_send)
    )
    d_normed = normed_gradient(slice(None, home)) + after(d_normed_got, gate_sum).astype(F32)

    gain_two_sum = jnp.sum(d_normed * hat_two, axis=0)
    d_hat = d_normed * gain_two
    mean_two = jnp.mean(d_hat * hat_two, axis=1, keepdims=True)
    d_resid = (cotangent[:home].astype(F32) + scale_two * (d_hat - hat_two * mean_two)).astype(BF16)
    d_resid_span = in_order(part_low, d_resid, to_half(d_resid), 0)

    activated_late, output_late = after(activated, d_resid), after(output_got, d_resid)
    output_own = dot(activated_late[:home], down_mine) + cols_of(resid_mid, slot, half_width)
    output_own = (output_own + output_late[home:].astype(F32)).astype(BF16)
    output_other = dot(activated_late[home:], down_mine) + after(resid_got, d_resid).astype(F32)
    output_other = (output_other + output_late[:home].astype(F32)).astype(BF16)
    output_half = in_order(part_low, output_own, output_other, 0)
    up_sum = finish(dot_tn(after(low, output_other), up_mine), up_core[:half_width], after(up_col, output_other))

    d_gated = dot_nt(d_resid_span, mixer_out)
    d_cproj = (d_gated * conved).astype(BF16)
    d_conved = d_gated * c_proj
    first_term = mask_one * d_conved
    second = mask_two * d_conved
    edge = to_core(jnp.concatenate([first_term[:edge_rows], second[:edge_rows]], axis=0))
    edge = jnp.where(core_low, swap_halves(edge, 1), 0.0)
    from_behind = kernel[1] * pad_rows(edge[:1], edge_rows - 1, 0) + kernel[2] * pad_rows(
        edge[edge_rows : edge_rows + 2], edge_rows - 2, 0
    )
    d_mixed = (
        kernel[0] * d_conved
        + kernel[1] * pad_rows(first_term[1:], 0, 1)
        + kernel[2] * pad_rows(second[2:], 0, 2)
        + pad_rows(from_behind, rest, 0)
    )
    kernel_sum = jnp.stack(
        [
            jnp.sum(d_conved * mixed_in, axis=0),
            jnp.sum(first_term * lag_one, axis=0) + jnp.sum(first_term[:edge_rows] * before_one, axis=0),
            jnp.sum(second * lag_two, axis=0) + jnp.sum(second[:edge_rows] * before_two, axis=0),
        ]
    )
    d_bproj = (d_mixed * x_proj).astype(BF16)
    d_xproj = (d_mixed * b_proj).astype(BF16)
    d_projected = jnp.stack([d_bproj, d_cproj, d_xproj])

    gated_late = after(gated_out, d_resid_span)
    out_core = to_core(dot_tn(gated_late[:, channels:], d_resid_span).astype(BF16))
    gated_mine = gated_late[:, :channels]
    out_high = dot_tn(gated_mine, d_resid_span[:, half_width:])
    out_high = (out_high + out_core[:, half_width:].astype(F32)).astype(BF16)
    out_col = to_col(out_high)

    def in_piece(left, pieces):
        return jnp.einsum("td,jtc->jdc", left, pieces, preferred_element_type=F32)

    in_core = to_core(in_piece(normed_one, d_projected[:, :, channels:]).astype(BF16))
    mine = d_projected[:, :, :channels]
    in_high = in_piece(normed_one[:, half_width:], mine)
    in_high = (in_high + in_core[:, half_width:].astype(F32)).astype(BF16)
    in_col = to_col(in_high)

    mixer_in_late = after(mixer_in, d_resid)

    def input_gradient(values, index):
        weights = lax.dynamic_slice_in_dim(mixer_in_late, index * half_width, half_width, axis=1)
        return jnp.einsum("jtc,jdc->td", values, weights, preferred_element_type=F32)

    d_projected_late = after(d_projected, in_high)
    one_send = input_gradient(d_projected_late, 1 - slot).astype(BF16)
    one_got = to_half(one_send)
    out_sum = finish(
        dot_tn(gated_mine, after(d_resid_span, one_send)[:, :half_width]),
        out_core[:, :half_width],
        out_col,
    )
    in_low = in_piece(after(normed_one[:, :half_width], one_send), mine)
    in_low = in_low + in_core[:, :half_width].astype(F32)
    d_normed_one = input_gradient(d_projected_late, slot) + one_got.astype(F32)

    block_output = scatter_span(after(output_half, one_send))

    hat_one = input_half.astype(F32) * scale_one
    gain_half = lax.dynamic_slice_in_dim(mixer_norm_gain, part * half_width, half_width)
    gain_one_sum = jnp.sum(d_normed_one * hat_one, axis=0)
    d_hat_one = d_normed_one * gain_half
    stat = jnp.sum(d_hat_one * hat_one, axis=1)
    mean_one = ((stat + to_half(stat)) / width)[:, None]
    d_input = cols_of(d_resid_span, slot, half_width).astype(F32) + scale_one * (d_hat_one - hat_one * mean_one)
    block_input_gradient = scatter_span(d_input)

    grad_down, _, _ = line_sum(down_sum, BF16, (d_resid,), (in_high,))
    grad_gate, _, _ = line_sum(gate_sum, BF16, (d_resid_span,), (d_normed_one,))
    grad_up, _, up_whole = line_sum(up_sum, BF16, (one_send,), (d_input,))
    grad_out, out_half, out_whole = line_sum(out_sum, BF16, (d_input,), (up_whole,))
    in_sum = in_low + in_col.astype(F32)
    grad_in, in_half, in_whole = line_sum(in_sum, BF16, (d_input, out_half), (out_whole,))

    kernel_sum = jnp.where(core_low, kernel_sum, swap_halves(kernel_sum, 1))
    halves = jnp.concatenate([kernel_sum, gain_one_sum[None]], axis=0)
    wide = in_order(part_low, halves, jnp.zeros_like(halves), 1)
    two = gain_two_sum[None]
    small = jnp.concatenate([wide, jnp.where(col_low, two, swap_halves(two, 1))], axis=0)
    small = small + to_core(small)
    small = small + to_col(small)
    small = small + to_half(small)
    small = line_sum(small, F32, (in_half,), (in_whole,))[0]
    small = lax.dynamic_slice_in_dim(small, (row * 2 + col) * own_width, own_width, axis=1)

    return (
        block_output,
        block_input_gradient,
        grad_in,
        grad_out,
        grad_gate,
        grad_up,
        grad_down,
        small[:3],
        small[3],
        small[4],
    )


def solution(mesh):
    placed = (
        P("dp", None, ("row", "col")),
        P("dp", None),
        P("dp", None, ("row", "col")),
        P(None, "col", "row"),
        P("row", "col"),
        P("col", "row"),
        P("col", "row"),
        P("row", "col"),
        P(None, ("row", "col")),
        P(),
        P(),
    )
    return jax.shard_map(
        body,
        mesh=mesh,
        in_specs=placed,
        out_specs=(
            P("dp", None, ("row", "col")),
            P("dp", None, ("row", "col")),
            P(None, "col", "row"),
            P("row", "col"),
            P("col", "row"),
            P("col", "row"),
            P("row", "col"),
            P(None, ("row", "col")),
            P(("row", "col")),
            P(("row", "col")),
        ),
        check_vma=False,
    )
```

```python
import jax
import jax.numpy as jnp
from jax import lax
from jax.sharding import PartitionSpec as P


EPS = 1e-05
F32 = jnp.float32
BF16 = jnp.bfloat16


def contract(left, right, left_axis, right_axis):
    return lax.dot_general(
        left, right, (((left_axis,), (right_axis,)), ((), ())), preferred_element_type=F32
    )


def dot(left, right):
    return contract(left, right, 1, 0)


def dot_nt(left, right):
    return contract(left, right, 1, 1)


def dot_tn(left, right):
    return contract(left, right, 0, 0)


def rounded(values):
    return lax.reduce_precision(values, exponent_bits=8, mantissa_bits=7)


def in_order(first_is_mine, mine, other, axis):
    return jnp.where(
        first_is_mine,
        jnp.concatenate([mine, other], axis=axis),
        jnp.concatenate([other, mine], axis=axis),
    )


def swap_halves(values, axis):
    low, high = jnp.split(values, 2, axis=axis)
    return jnp.concatenate([high, low], axis=axis)


def rows_of(values, index, count):
    return lax.dynamic_slice_in_dim(values, index * count, count, axis=0)


def cols_of(values, index, count):
    return lax.dynamic_slice_in_dim(values, index * count, count, axis=1)


def after(values, *others):
    return lax.optimization_barrier((values, *others))[0]


def pad_rows(values, before, behind):
    return jnp.pad(values, ((before, behind), (0, 0)))


def to_col(values):
    size = lax.axis_size("col")
    return lax.ppermute(values, "col", [(i, size - 1 - i) for i in range(size)])


def to_core(values):
    size = lax.axis_size("row")
    return lax.ppermute(values, "row", [(i, i ^ 1) for i in range(size)])


def to_half(values):
    size = lax.axis_size("row")
    return lax.ppermute(values, "row", [(i, (i + size // 2) % size) for i in range(size)])


def line_sum(values, dtype, middle_after=(), outward_after=()):
    size = lax.axis_size("dp")
    place = lax.axis_index("dp")
    middle = size // 2
    keep = rounded if dtype == BF16 else (lambda v: v)
    total = values
    for step in range(middle - 1):
        pairs = [(step, step + 1), (size - 1 - step, size - 2 - step)]
        got = after(lax.ppermute(keep(total).astype(dtype), "dp", pairs), *middle_after)
        total = total + got.astype(F32)
    half = keep(total).astype(dtype)
    pairs = [(middle - 1, middle), (middle, middle - 1)]
    got = after(lax.ppermute(half, "dp", pairs), *outward_after)
    whole = keep(keep(total) + got.astype(F32)).astype(dtype)

    def outward(*end_after):
        result = whole
        for step in range(middle - 1):
            pairs = [(middle - 1 - step, middle - 2 - step), (middle + step, middle + step + 1)]
            got = after(lax.ppermute(result, "dp", pairs), *end_after)
            taker = (place == middle - 2 - step) | (place == middle + step + 1)
            result = jnp.where(taker, got, result)
        return result.astype(F32)

    return outward, half, whole


def body(
    block_input,
    segment_ids,
    out_grad,
    in_weight,
    out_weight,
    gate_weight,
    up_weight,
    down_weight,
    conv_weight,
    mixer_norm_gain,
    feedforward_norm_gain,
):
    seq_count, seq_length, own_width = block_input.shape
    if lax.axis_size("row") != 4 or lax.axis_size("col") != 2 or seq_count != 2 or lax.axis_size("dp") % 2:
        raise ValueError("unsupported mesh")
    row = lax.axis_index("row")
    col = lax.axis_index("col")
    part = row >> 1
    core = row & 1
    span = seq_length // 2
    home = span // 2
    width = mixer_norm_gain.shape[0]
    half_width = width // 2
    own_half_first = part == col
    core_low = core == 0
    part_low = part == 0
    col_low = col == 0

    def local_gain(gain):
        return jnp.concatenate(
            [
                lax.dynamic_slice_in_dim(gain, col * half_width, half_width),
                lax.dynamic_slice_in_dim(gain, (1 - col) * half_width, half_width),
            ]
        )

    def scatter_span(values):
        wide = 2 * own_width
        mine = cols_of(values, core, wide)
        got = to_core(cols_of(values, 1 - core, wide).astype(BF16)).astype(values.dtype)
        pair = in_order(core_low, mine, got, 0)
        mine = cols_of(pair, col, own_width)
        got = to_col(cols_of(pair, 1 - col, own_width).astype(BF16)).astype(values.dtype)
        return in_order(col_low, mine[None], got[None], 0)

    def local_features(mine, other):
        return jnp.concatenate(
            [jnp.where(own_half_first, mine, other), jnp.where(own_half_first, other, mine)], axis=1
        )

    def of_sequence(values, index):
        return lax.dynamic_index_in_dim(values, index, 0, keepdims=False)

    def gather_span(values, got):
        pair = in_order(col_low, of_sequence(values, col), got, 1)
        got = to_core(rows_of(pair, 1 - core, span))
        quad = in_order(core_low, rows_of(pair, core, span), got, 1)
        return quad, to_half(quad)

    input_got = to_col(of_sequence(block_input, 1 - col))
    input_half, input_other = gather_span(block_input, input_got)

    mixer_in = jnp.concatenate([in_weight, to_col(in_weight)], axis=1)
    mixer_in = jnp.concatenate([mixer_in, to_core(mixer_in)], axis=2)
    mixer_out = jnp.concatenate([out_weight, to_col(out_weight)], axis=1)
    mixer_out = jnp.concatenate([mixer_out, to_core(mixer_out)], axis=0)
    kernel = in_order(col_low, conv_weight, to_col(conv_weight), 1)
    kernel = jnp.concatenate([kernel, to_core(kernel)], axis=1).astype(F32)

    gate_got = to_col(gate_weight)
    cot_got = to_col(of_sequence(out_grad, 1 - col))
    up_got, down_got = to_col(up_weight), to_col(down_weight)
    hidden = gate_weight.shape[1]
    channels = in_weight.shape[2]

    gain_one = local_gain(mixer_norm_gain)
    gain_two = local_gain(feedforward_norm_gain)

    segments = lax.dynamic_index_in_dim(segment_ids, col, 0, keepdims=False)

    def same_as(lag):
        earlier = jnp.concatenate([jnp.full((lag,), -1, jnp.int32), segments[:-lag]])
        return rows_of(jnp.where(earlier == segments, 1.0, 0.0).astype(F32), core, span)[:, None]

    mask_one, mask_two = same_as(1), same_as(2)

    inputs = local_features(input_half, input_other).astype(F32)
    scale_one = lax.rsqrt(jnp.mean(inputs * inputs, axis=1, keepdims=True) + EPS)
    normed_one = (inputs * scale_one * gain_one).astype(BF16)
    projected = jnp.einsum("td,jdc->jtc", normed_one, mixer_in, preferred_element_type=F32)
    b_proj, c_proj, x_proj = projected[0], projected[1], projected[2]
    mixed_in = b_proj * x_proj
    edge_rows = 8
    rest = span - edge_rows
    before = jnp.where(core_low, 0.0, swap_halves(to_core(mixed_in[rest:]), 1))
    before_one = pad_rows(before[edge_rows - 1 :], 0, edge_rows - 1)
    before_two = pad_rows(before[edge_rows - 2 :], 0, edge_rows - 2)
    lag_one, lag_two = pad_rows(mixed_in[:-1], 1, 0), pad_rows(mixed_in[:-2], 2, 0)
    from_before = (
        kernel[1] * mask_one[:edge_rows] * before_one + kernel[2] * mask_two[:edge_rows] * before_two
    )
    conved = (
        kernel[0] * mixed_in
        + kernel[1] * mask_one * lag_one
        + kernel[2] * mask_two * lag_two
        + pad_rows(from_before, 0, rest)
    )
    gated_out = (c_proj * conved).astype(BF16)
    mixer_send = dot(rows_of(gated_out, 1 - part, home), mixer_out).astype(BF16)
    mixer_got = to_half(mixer_send)
    gate_all = jnp.concatenate([gate_weight, after(gate_got, mixer_send)], axis=0)
    gate_all = jnp.concatenate([gate_all, to_core(gate_all)], axis=1)
    resid_mid = rows_of(inputs, part, home) + dot(rows_of(gated_out, part, home), mixer_out) + mixer_got.astype(F32)

    scale_two = lax.rsqrt(jnp.mean(resid_mid * resid_mid, axis=1, keepdims=True) + EPS)
    hat_two = resid_mid * scale_two
    normed_own = (hat_two * gain_two).astype(BF16)
    normed_other = to_half(normed_own)
    cot_half, cot_other = gather_span(out_grad, after(cot_got, normed_own))
    normed_two = jnp.concatenate([normed_own, normed_other], axis=0)
    slot = jnp.where(own_half_first, 0, 1)
    resid_got = to_half(cols_of(resid_mid, 1 - slot, half_width).astype(BF16))
    gate_pre = dot(normed_two, gate_all)
    up_all = jnp.concatenate([up_weight, after(up_got, gate_pre)], axis=0)
    up_all = jnp.concatenate([up_all, to_core(up_all)], axis=1)
    up_pre = dot(normed_two, up_all)
    sigmoid = jax.nn.sigmoid(gate_pre)
    activated = (gate_pre * sigmoid * up_pre).astype(BF16)
    down_all = jnp.concatenate([down_weight, after(down_got, activated)], axis=1)
    down_all = jnp.concatenate([down_all, to_core(down_all)], axis=0)
    cot_span = local_features(cot_half, after(cot_other, activated))
    cotangent = jnp.concatenate([rows_of(cot_span, part, home), rows_of(cot_span, 1 - part, home)], axis=0)

    def finish(low, from_core, from_col):
        return low + from_core.astype(F32) + from_col.astype(F32)

    down_core = to_core(dot_tn(activated[:, hidden:], cotangent).astype(BF16))
    activated_mine = activated[:, :hidden]
    down_high = dot_tn(activated_mine, cotangent[:, half_width:])
    down_high = (down_high + down_core[:, half_width:].astype(F32)).astype(BF16)
    down_col = to_col(down_high)

    down_mine = cols_of(down_all, slot, half_width)
    down_other = cols_of(down_all, 1 - slot, half_width)
    output_send = dot(activated, down_other).astype(BF16)
    output_got = to_half(output_send)

    d_act = dot_nt(after(cotangent, down_high, output_send), down_all)
    d_up = (d_act * gate_pre * sigmoid).astype(BF16)
    d_gate = (d_act * up_pre * sigmoid * (1.0 + gate_pre * (1.0 - sigmoid))).astype(BF16)

    low, high = normed_two[:, :half_width], normed_two[:, half_width:]
    gate_core = to_core(dot_tn(normed_two, d_gate[:, hidden:]).astype(BF16))
    up_core = to_core(dot_tn(normed_two, d_up[:, hidden:]).astype(BF16))
    gate_mine, up_mine = d_gate[:, :hidden], d_up[:, :hidden]
    gate_high = dot_tn(high, gate_mine)
    gate_high = (gate_high + gate_core[half_width:].astype(F32)).astype(BF16)
    gate_col = to_col(gate_high)
    up_high = (dot_tn(high, up_mine) + up_core[half_width:].astype(F32)).astype(BF16)
    up_col = to_col(up_high)

    down_sum = finish(
        dot_tn(activated_mine, after(cotangent, up_high)[:, :half_width]),
        down_core[:, :half_width],
        after(down_col, up_high),
    )

    d_gate_late, d_up_late = after(d_gate, up_high), after(d_up, up_high)

    def normed_gradient(rows):
        return dot_nt(d_gate_late[rows], gate_all) + dot_nt(d_up_late[rows], up_all)

    d_normed_send = normed_gradient(slice(home, None)).astype(BF16)
    d_normed_got = to_half(d_normed_send)
    gate_sum = finish(
        dot_tn(after(low, d_normed_send), gate_mine), gate_core[:half_width], after(gate_col, d_normed_send)
    )
    d_normed = normed_gradient(slice(None, home)) + after(d_normed_got, gate_sum).astype(F32)

    gain_two_sum = jnp.sum(d_normed * hat_two, axis=0)
    d_hat = d_normed * gain_two
    mean_two = jnp.mean(d_hat * hat_two, axis=1, keepdims=True)
    d_resid = (cotangent[:home].astype(F32) + scale_two * (d_hat - hat_two * mean_two)).astype(BF16)
    d_resid_span = in_order(part_low, d_resid, to_half(d_resid), 0)

    activated_late, output_late = after(activated, d_resid), after(output_got, d_resid)
    output_own = dot(activated_late[:home], down_mine) + cols_of(resid_mid, slot, half_width)
    output_own = (output_own + output_late[home:].astype(F32)).astype(BF16)
    output_other = dot(activated_late[home:], down_mine) + after(resid_got, d_resid).astype(F32)
    output_other = (output_other + output_late[:home].astype(F32)).astype(BF16)
    output_half = in_order(part_low, output_own, output_other, 0)
    up_sum = finish(dot_tn(after(low, output_other), up_mine), up_core[:half_width], after(up_col, output_other))

    d_gated = dot_nt(d_resid_span, mixer_out)
    d_cproj = (d_gated * conved).astype(BF16)
    d_conved = d_gated * c_proj
    first_term = mask_one * d_conved
    second = mask_two * d_conved
    edge = to_core(jnp.concatenate([first_term[:edge_rows], second[:edge_rows]], axis=0))
    edge = jnp.where(core_low, swap_halves(edge, 1), 0.0)
    from_behind = kernel[1] * pad_rows(edge[:1], edge_rows - 1, 0) + kernel[2] * pad_rows(
        edge[edge_rows : edge_rows + 2], edge_rows - 2, 0
    )
    d_mixed = (
        kernel[0] * d_conved
        + kernel[1] * pad_rows(first_term[1:], 0, 1)
        + kernel[2] * pad_rows(second[2:], 0, 2)
        + pad_rows(from_behind, rest, 0)
    )
    kernel_sum = jnp.stack(
        [
            jnp.sum(d_conved * mixed_in, axis=0),
            jnp.sum(first_term * lag_one, axis=0) + jnp.sum(first_term[:edge_rows] * before_one, axis=0),
            jnp.sum(second * lag_two, axis=0) + jnp.sum(second[:edge_rows] * before_two, axis=0),
        ]
    )
    d_bproj = (d_mixed * x_proj).astype(BF16)
    d_xproj = (d_mixed * b_proj).astype(BF16)
    d_projected = jnp.stack([d_bproj, d_cproj, d_xproj])

    gated_late = after(gated_out, d_resid_span)
    out_core = to_core(dot_tn(gated_late[:, channels:], d_resid_span).astype(BF16))
    gated_mine = gated_late[:, :channels]
    out_high = dot_tn(gated_mine, d_resid_span[:, half_width:])
    out_high = (out_high + out_core[:, half_width:].astype(F32)).astype(BF16)
    out_col = to_col(out_high)

    def in_piece(left, pieces):
        return jnp.einsum("td,jtc->jdc", left, pieces, preferred_element_type=F32)

    in_core = to_core(in_piece(normed_one, d_projected[:, :, channels:]).astype(BF16))
    mine = d_projected[:, :, :channels]
    in_high = in_piece(normed_one[:, half_width:], mine)
    in_high = (in_high + in_core[:, half_width:].astype(F32)).astype(BF16)
    in_col = to_col(in_high)

    mixer_in_late = after(mixer_in, d_resid)

    def input_gradient(values, index):
        weights = lax.dynamic_slice_in_dim(mixer_in_late, index * half_width, half_width, axis=1)
        return jnp.einsum("jtc,jdc->td", values, weights, preferred_element_type=F32)

    d_projected_late = after(d_projected, in_high)
    one_send = input_gradient(d_projected_late, 1 - slot).astype(BF16)
    one_got = to_half(one_send)
    out_sum = finish(
        dot_tn(gated_mine, after(d_resid_span, one_send)[:, :half_width]),
        out_core[:, :half_width],
        out_col,
    )
    in_low = in_piece(after(normed_one[:, :half_width], one_send), mine)
    in_low = in_low + in_core[:, :half_width].astype(F32)
    d_normed_one = input_gradient(d_projected_late, slot) + one_got.astype(F32)

    block_output = scatter_span(after(output_half, one_send))

    hat_one = input_half.astype(F32) * scale_one
    gain_half = lax.dynamic_slice_in_dim(mixer_norm_gain, part * half_width, half_width)
    gain_one_sum = jnp.sum(d_normed_one * hat_one, axis=0)
    d_hat_one = d_normed_one * gain_half
    stat = jnp.sum(d_hat_one * hat_one, axis=1)
    mean_one = ((stat + to_half(stat)) / width)[:, None]
    d_input = cols_of(d_resid_span, slot, half_width).astype(F32) + scale_one * (d_hat_one - hat_one * mean_one)
    block_input_gradient = scatter_span(d_input)

    in_sum = in_low + in_col.astype(F32)
    late = (d_input,)
    up_out, up_half, up_whole = line_sum(up_sum, BF16, (one_send,), late)
    out_out, out_half, out_whole = line_sum(out_sum, BF16, late, (up_whole,))
    in_out, in_half, in_whole = line_sum(in_sum, BF16, (d_input, out_half), (out_whole,))
    down_out, _, _ = line_sum(down_sum, BF16, (d_resid,), (d_cproj,))
    gate_out, _, _ = line_sum(gate_sum, BF16, (d_resid_span,), (up_half,))
    grad_down, grad_gate = down_out(d_input, out_half), gate_out(in_half)
    grad_up, grad_out, grad_in = up_out(in_whole), out_out(in_whole), in_out()

    kernel_sum = jnp.where(core_low, kernel_sum, swap_halves(kernel_sum, 1))
    halves = jnp.concatenate([kernel_sum, gain_one_sum[None]], axis=0)
    wide = in_order(part_low, halves, jnp.zeros_like(halves), 1)
    two = gain_two_sum[None]
    small = jnp.concatenate([wide, jnp.where(col_low, two, swap_halves(two, 1))], axis=0)
    small = small + to_core(small)
    small = small + to_col(small)
    small = small + to_half(small)
    small = line_sum(small, F32, (in_whole,))[0]()
    small = lax.dynamic_slice_in_dim(small, (row * 2 + col) * own_width, own_width, axis=1)

    return (
        block_output,
        block_input_gradient,
        grad_in,
        grad_out,
        grad_gate,
        grad_up,
        grad_down,
        small[:3],
        small[3],
        small[4],
    )


def solution(mesh):
    placed = (
        P("dp", None, ("row", "col")),
        P("dp", None),
        P("dp", None, ("row", "col")),
        P(None, "col", "row"),
        P("row", "col"),
        P("col", "row"),
        P("col", "row"),
        P("row", "col"),
        P(None, ("row", "col")),
        P(),
        P(),
    )
    return jax.shard_map(
        body,
        mesh=mesh,
        in_specs=placed,
        out_specs=(
            P("dp", None, ("row", "col")),
            P("dp", None, ("row", "col")),
            P(None, "col", "row"),
            P("row", "col"),
            P("col", "row"),
            P("col", "row"),
            P("row", "col"),
            P(None, ("row", "col")),
            P(("row", "col")),
            P(("row", "col")),
        ),
        check_vma=False,
    )
```
